512 devices in a mesh: group: 8 (over z), shard: 16 (over y, x_lo), tensor: 4 (over x_hi, core).
Axes of the slice: x: 4 (x_hi: 2, x_lo: 2; x = x_hi * 2 + x_lo), y: 8, z: 8, core: 2. Of those that a mesh axis runs over, the one named last changes fastest.
Arguments:
- attn_in_local: bfloat16 [8, 768, 2304], P('group', 'shard', 'tensor'), may hold values from -6 to 6
- attn_out_local: bfloat16 [8, 768, 768], P('group', 'shard', 'tensor'), may hold values from -6 to 6
- ffn_in_local: bfloat16 [8, 768, 3072], P('group', 'shard', 'tensor'), may hold values from -6 to 6
- ffn_out_local: bfloat16 [8, 3072, 768], P('group', 'shard', 'tensor'), may hold values from -6 to 6
- small_local: bfloat16 [8, 1920], P('group'), may hold values from -6 to 6
- dense_old: float32 [64, 110592], P(('shard', 'tensor'), 'group'), may hold values from -6 to 6
- dense_momentum: float32 [64, 110592], P(('shard', 'tensor'), 'group'), may hold values from -6 to 6
- small_old: float32 [1920], P('group'), may hold values from -6 to 6
- small_momentum: float32 [1920], P('group'), may hold values from -6 to 6
- embed_local: bfloat16 [8, 768, 8192], P('group', 'shard', 'tensor'), may hold values from -6 to 6
- embed_old: float32 [768, 8192], P('shard', 'tensor'), may hold values from -6 to 6
- basis: float32 [768, 64], P('shard'), may hold values from -0.21875 to 0.21875
- coeff_momentum: float32 [64, 8192], P(None, 'tensor'), may hold values from -6 to 6
Outputs:
- attn_in_next: float32 [768, 2304], P('shard', 'tensor')
- attn_out_next: float32 [768, 768], P('shard', 'tensor')
- ffn_in_next: float32 [768, 3072], P('shard', 'tensor')
- ffn_out_next: float32 [3072, 768], P('shard', 'tensor')
- dense_momentum_next: float32 [64, 110592], P(('shard', 'tensor'), 'group')
- small_next: float32 [1920], replicated
- small_momentum_next: float32 [1920], P('group')
- embed_next: float32 [768, 8192], P('shard', 'tensor')
- coeff_momentum_next: float32 [64, 8192], P(None, 'tensor')
The draws below stay inside these ranges and needn't reach their ends.
All inputs are finite; a program needn't handle non-finite values.
Results may differ from the reference program's by a relative error of at most 0.0003.
Values sent between devices are 32-bit elements; how exact they have to be, the bound alone decides.
A program may use at most 64 MiB of HBM per device.

```python
import jax
import jax.numpy as jnp
from jax import lax

D = 768
FF = 3072
VOCAB = 8192
RANK = 64
SMALL = 1920
SHARDS = 64
FLAT = 110592
N_GROUP = 8
N_SHARD = 16
N_TENSOR = 4


def level_of(own_key, extent, shards, least, top_value):
    factor_of, own = 1.0, jax.random.fold_in(own_key, 6)
    for dim, parts in shards:
        steps = jnp.exp(jax.random.uniform(jax.random.fold_in(own, dim), (parts,), jnp.float32, least / len(shards), top_value / len(shards)))
        factor_of = factor_of * jnp.repeat(steps, extent[dim] // parts).reshape([-1 if axis == dim else 1 for axis in range(len(extent))])
    return factor_of


def bell_draw(stream_key, dims, width, limit, cuts=(), kind=jnp.bfloat16):
    drawn = width * jax.random.normal(stream_key, dims, jnp.float32)
    if cuts:
        drawn = drawn * level_of(stream_key, dims, cuts, -0.22, 0.18)
    return jnp.clip(drawn, -limit, limit).astype(kind)


def setup_inputs(seed: int = 0) -> dict:
    key_of = jax.random.split(jax.random.key(seed), 14)
    return {
        "attn_in_local": bell_draw(key_of[0], (N_GROUP, D, 3 * D), 1.0, 6.0, ((0, 8), (1, 16), (2, 4))),
        "attn_out_local": bell_draw(key_of[1], (N_GROUP, D, D), 1.0, 6.0, ((0, 8), (1, 16), (2, 4))),
        "ffn_in_local": bell_draw(key_of[2], (N_GROUP, D, FF), 1.0, 6.0, ((0, 8), (1, 16), (2, 4))),
        "ffn_out_local": bell_draw(key_of[3], (N_GROUP, FF, D), 1.0, 6.0, ((0, 8), (1, 16), (2, 4))),
        "small_local": bell_draw(key_of[4], (N_GROUP, SMALL), 1.0, 6.0, ((0, 8),)),
        "dense_old": bell_draw(key_of[5], (SHARDS, FLAT), 1.0, 6.0, ((0, 64), (1, 8)), jnp.float32),
        "dense_momentum": bell_draw(key_of[6], (SHARDS, FLAT), 1.0, 6.0, ((0, 64), (1, 8)), jnp.float32),
        "small_old": bell_draw(key_of[7], (SMALL,), 1.0, 6.0, ((0, 8),), jnp.float32),
        "small_momentum": bell_draw(key_of[8], (SMALL,), 1.0, 6.0, ((0, 8),), jnp.float32),
        "embed_local": bell_draw(key_of[9], (N_GROUP, D, VOCAB), 1.0, 6.0, ((0, 8), (1, 16), (2, 4))),
        "embed_old": bell_draw(key_of[10], (D, VOCAB), 1.0, 6.0, ((0, 16), (1, 4)), jnp.float32),
        "basis": bell_draw(key_of[11], (D, RANK), D ** -0.5, 0.21875, ((0, 16),), jnp.float32),
        "coeff_momentum": bell_draw(key_of[12], (RANK, VOCAB), 1.0, 6.0, ((1, 4),), jnp.float32),
    }


momentum_coef = 0.5
outer_rate = 0.7


def flatten_shards(matrices):
    pieces = []
    for matrix in matrices:
        row_count, col_count = matrix.shape
        blocks = matrix.reshape(N_SHARD, row_count // N_SHARD, N_TENSOR, col_count // N_TENSOR).transpose(0, 2, 1, 3)
        pieces.append(blocks.reshape(N_SHARD * N_TENSOR, -1))
    return jnp.concatenate(pieces, axis=1)


def unflatten_shards(flat, shapes):
    results = []
    offset = 0
    for row_count, col_count in shapes:
        block_size = (row_count // N_SHARD) * (col_count // N_TENSOR)
        piece = flat[:, offset:offset + block_size].reshape(N_SHARD, N_TENSOR, row_count // N_SHARD, col_count // N_TENSOR)
        results.append(piece.transpose(0, 2, 1, 3).reshape(row_count, col_count))
        offset = offset + block_size
    return results


def nesterov(old_value, momentum, delta):
    moved = momentum_coef * momentum + delta
    return old_value - outer_rate * (delta + momentum_coef * moved), moved


def reference(attn_in_local, attn_out_local, ffn_in_local, ffn_out_local, small_local, dense_old, dense_momentum, small_old, small_momentum, embed_local, embed_old, basis, coeff_momentum):
    dense_total = jnp.zeros(dense_old.shape, jnp.float32)
    small_total = jnp.zeros(small_old.shape, jnp.float32)
    coeff_total = jnp.zeros(coeff_momentum.shape, jnp.float32)
    for member in range(N_GROUP):
        flat = flatten_shards([attn_in_local[member], attn_out_local[member], ffn_in_local[member], ffn_out_local[member]])
        dense_total = dense_total + flat.astype(jnp.float32)
        small_total = small_total + small_local[member].astype(jnp.float32)
        difference = embed_old - embed_local[member].astype(jnp.float32)
        coeff_total = coeff_total + jnp.dot(basis.T, difference, precision=lax.Precision.HIGHEST, preferred_element_type=jnp.float32)
    dense_new, dense_moved = nesterov(dense_old, dense_momentum, dense_old - dense_total / N_GROUP)
    small_new, small_moved = nesterov(small_old, small_momentum, small_old - small_total / N_GROUP)
    shapes = [attn_in_local.shape[1:], attn_out_local.shape[1:], ffn_in_local.shape[1:], ffn_out_local.shape[1:]]
    attn_in_next, attn_out_next, ffn_in_next, ffn_out_next = unflatten_shards(dense_new, shapes)
    coeff = coeff_total / N_GROUP
    coeff_moved = momentum_coef * coeff_momentum + coeff
    update = coeff + momentum_coef * coeff_moved
    embed_next = embed_old - outer_rate * jnp.dot(basis, update, precision=lax.Precision.HIGHEST, preferred_element_type=jnp.float32)
    return (attn_in_next, attn_out_next, ffn_in_next, ffn_out_next, dense_moved, small_new, small_moved, embed_next, coeff_moved)
```

```python
import functools

import jax
import jax.numpy as jnp
from jax import lax
from jax.experimental import pallas as pl
from jax.experimental.pallas import tpu as pltpu
from jax.sharding import PartitionSpec as P

momentum_coef = 0.5
outer_rate = 0.7

MESH = pl.DeviceIdType.MESH
F32 = jnp.float32
BF16 = jnp.bfloat16

NZ = 8
NY = 8
NX = 2
ROWS = 112
DENSE_ROWS = 108
RANK = 64
Q = 2

PLAN = (
    (0, 0, 0, 24, 0),
    (0, 1, 24, 24, 0),
    (1, 2, 0, 48, 0),
    (2, 2, 0, 6, 72),
    (2, 3, 6, 18, 0),
    (2, 4, 24, 18, 0),
    (2, 5, 42, 6, 0),
    (3, 5, 0, 48, 36),
    (3, 6, 48, 72, 0),
    (3, 7, 120, 72, 0),
)
WIDTHS = (576, 192, 768, 192)
HEIGHTS = (48, 48, 48, 192)
TILES = tuple(-(-width // 128) for width in WIDTHS)


def nesterov(old_value, momentum, delta):
    moved = momentum_coef * momentum + delta
    return (old_value - outer_rate * (delta + momentum_coef * moved), moved)


def lower_lanes(shape):
    return lax.broadcasted_iota(jnp.int32, shape, 1) < 64


def pack(tiles, flat):
    for which, owner, row, count, base in PLAN:
        xs = tiles[which]
        full = WIDTHS[which] // 128
        if WIDTHS[which] % 128 == 0:
            for t in range(full):
                flat[owner, pl.ds(base + t, count, stride=full), :] = xs[t, pl.ds(row, count), :]
            continue
        n, step = count // 2, 2 * full + 1
        low = lower_lanes((n, 128))
        even = [xs[t, pl.ds(row, n, stride=2), :] for t in range(full + 1)]
        turned = [
            pltpu.roll(xs[t, pl.ds(row + 1, n, stride=2), :], 64, 1) for t in range(full + 1)
        ]
        for t in range(full):
            flat[owner, pl.ds(base + t, n, stride=step), :] = even[t]
        flat[owner, pl.ds(base + full, n, stride=step), :] = jnp.where(low, even[full], turned[0])
        for t in range(full):
            flat[owner, pl.ds(base + full + 1 + t, n, stride=step), :] = jnp.where(
                low, turned[t], turned[t + 1]
            )


def unpack(flat, tiles):
    for which, owner, row, count, base in PLAN:
        xs = tiles[which]
        full = WIDTHS[which] // 128
        if WIDTHS[which] % 128 == 0:
            for t in range(full):
                xs[t, pl.ds(row, count), :] = flat[owner, pl.ds(base + t, count, stride=full), :]
            continue
        n, step = count // 2, 2 * full + 1
        low = lower_lanes((n, 128))
        rows = [flat[owner, pl.ds(base + t, n, stride=step), :] for t in range(step)]
        for t in range(full + 1):
            xs[t, pl.ds(row, n, stride=2), :] = rows[t]
        for t in range(full):
            xs[t, pl.ds(row + 1, n, stride=2), :] = pltpu.roll(
                jnp.where(low, rows[full + 1 + t], rows[full + t]), 64, 1
            )
        xs[full, pl.ds(row + 1, n, stride=2), :] = pltpu.roll(rows[2 * full], 64, 1)


def split_bf16(value):
    high = value.astype(BF16)
    return high, (value - high.astype(F32)).astype(BF16)


def flows(n):
    long, short = n // 2, n - 1 - n // 2
    order = []
    for q in range(Q):
        order += [(0, q, 1, long), (1, q, -1, long)]
    for q in range(Q):
        order += [(1, q, 1, short), (0, q, -1, short)]
    return order


def comm_kernel(*refs):
    (ai, ao, fi, fo, sl, dold, dmom, sold, smom, el, eo, ba) = refs[:12]
    full_out, moved_out, cfull_out = refs[12:15]
    (
        ai_v, ao_v, fi_v, fo_v, sl_v, dold_v, dmom_v, sold_v, smom_v, el_v, eo_v, ba_v,
        ai_x, ao_x, fi_x, fo_x, old_x, mom_x,
        dpart, dslots, dfull, dmoved,
        cpart, cslots, cmine, cmid, ctile, cfull,
        load_sem, store_sem,
        zs_sem, zr_sem, zas_sem, zar_sem,
        ys_sem, yr_sem, yas_sem, yar_sem,
        ms_sem, mr_sem, mas_sem, mar_sem,
    ) = refs[15:]

    z = lax.axis_index("group")
    shard = lax.axis_index("shard")
    y = shard // NX
    x = lax.rem(shard, NX)

    def at_z(offset):
        return {"group": lax.rem(z + offset + NZ, NZ)}

    def at_y(offset):
        return {"shard": lax.rem(y + offset + NY, NY) * NX + x}

    def at_mid(dx, dz):
        return {"group": lax.rem(z + dz, NZ), "shard": y * NX + lax.rem(x + dx, NX)}

    peers = [(dx, dz) for dx in range(NX) for dz in range(NZ) if dx or dz]

    loads = []
    for i, (src, dst) in enumerate(
        (
            (el, el_v), (eo, eo_v), (ba, ba_v), (ai, ai_v), (ao, ao_v), (fi, fi_v), (fo, fo_v),
            (sl, sl_v), (dold, dold_v), (dmom, dmom_v), (sold, sold_v), (smom, smom_v),
        )
    ):
        copy = pltpu.make_async_copy(src, dst, load_sem.at[i])
        copy.start()
        loads.append(copy)

    barrier = pltpu.get_barrier_semaphore()
    greeted = [at_y(1), at_y(-1)] + [at_mid(dx, dz) for dx, dz in peers]
    for peer in greeted:
        pl.semaphore_signal(barrier, inc=1, device_id=peer, device_id_type=MESH)

    for copy in loads[:3]:
        copy.wait()
    b_high, b_low = split_bf16(ba_v[...])
    left = jnp.concatenate([b_high, b_low, b_high, b_low], axis=0)

    for t in range(NY):
        c = lax.rem(y + 4 + t, NY)
        columns = pl.ds(pl.multiple_of(c * 256, 256), 256)
        high, low = split_bf16(eo_v[:, columns] - el_v[0, :, columns].astype(F32))
        right = jnp.concatenate([high, high, low, low], axis=0)
        product = lax.dot_general(
            left, right, (((0,), (0,)), ((), ())), preferred_element_type=F32
        )
        cpart[c, 0] = product[:, :128].reshape(NZ, 8, 128)
        cpart[c, 1] = product[:, 128:].reshape(NZ, 8, 128)

    pl.semaphore_wait(barrier, len(greeted))

    zflows, yflows = flows(NZ), flows(NY)
    zcuts = {}
    for half in range(2):
        bounds = (0, 32, 56) if Q == 2 else (0, 56)
        for q in range(Q):
            zcuts[half, q] = (half * 56 + bounds[q], bounds[q + 1] - bounds[q])

    def zpiece(ref, lead, half, q):
        start, size = zcuts[half, q]
        return ref.at[lead, pl.ds(start, size)]

    def ypiece(ref, lead, half, q):
        return ref.at[lead, half, pl.ds(q * (NZ // Q), NZ // Q)]

    sends = []

    def send(src, dst, send_sem, recv_sem, device):
        copy = pltpu.make_async_remote_copy(
            src_ref=src, dst_ref=dst, send_sem=send_sem, recv_sem=recv_sem,
            device_id=device, device_id_type=MESH,
        )
        copy.start()
        sends.append(copy)
        return copy

    def slot_of(f, s):
        return f * 4 + s

    rs_copies = {}

    def rs_send(axis, f, s):
        if axis == "z":
            half, q, way, hops = zflows[f]
            piece, part, slots, me, n, target = zpiece, dpart, dslots, z, NZ, at_z(way)
            ss, rr = zs_sem, zr_sem
        else:
            half, q, way, hops = yflows[f]
            piece, part, slots, me, n, target = ypiece, cpart, cslots, y, NY, at_y(way)
            ss, rr = ys_sem, yr_sem
        lead = 7 if way > 0 else 3
        del lead
        if s == 0:
            src = piece(part, lax.rem(me + way * hops + n, n), half, q)
        else:
            src = slot_ref(axis, f, s - 1)
        rs_copies[axis, f, s] = send(
            src, slot_ref(axis, f, s), ss.at[slot_of(f, s)], rr.at[slot_of(f, s)], target
        )

    def slot_ref(axis, f, s):
        half, q, way, hops = (zflows if axis == "z" else yflows)[f]
        lead = (0 if way > 0 else 4) + s
        if axis == "z":
            return zpiece(dslots, lead, half, q)
        return ypiece(cslots, lead, half, q)

    def rs_step(axis, f, s):
        half, q, way, hops = (zflows if axis == "z" else yflows)[f]
        rs_copies[axis, f, s].wait_recv()
        if s == hops - 1:
            return
        slot = slot_ref(axis, f, s)
        if axis == "z":
            own = zpiece(dpart, lax.rem(z + way * (hops - s - 1) + NZ, NZ), half, q)
        else:
            own = ypiece(cpart, lax.rem(y + way * (hops - s - 1) + NY, NY), half, q)
        slot[...] = slot[...] + own[...]
        rs_send(axis, f, s + 1)

    for f in range(len(yflows)):
        rs_send("y", f, 0)

    for copy in loads[3:]:
        copy.wait()
    for which, (src, dst) in enumerate(
        ((ai_v, ai_x), (ao_v, ao_x), (fi_v, fi_x), (fo_v, fo_x))
    ):
        for t in range(TILES[which]):
            size = min(128, WIDTHS[which] - 128 * t)
            dst[t, :, 0:size] = src[0, :, 128 * t : 128 * t + size].astype(F32)
    pack((ai_x, ao_x, fi_x, fo_x), dpart)
    small = sl_v[...].astype(F32)
    for owner in range(NZ):
        dpart[owner, 104:112, :] = jnp.where(
            lax.broadcasted_iota(jnp.int32, (8, 128), 0) < 4, dpart[owner, 104:112, :], 0.0
        )
        dpart[owner, 108:109, :] = small[:, 240 * owner : 240 * owner + 128]
        dpart[owner, 109:110, 0:112] = small[:, 240 * owner + 128 : 240 * owner + 240]

    for f in range(len(zflows)):
        rs_send("z", f, 0)

    for src, dst, small_src in ((dold_v, old_x, sold_v), (dmom_v, mom_x, smom_v)):
        dst[104:112, :] = jnp.zeros((8, 128), F32)
        for r in range(DENSE_ROWS):
            dst[r : r + 1, :] = src[:, 128 * r : 128 * r + 128]
        dst[108:109, :] = small_src[:, 0:128]
        dst[109:110, 0:112] = small_src[:, 128:240]

    for s in range(NZ // 2):
        for f in range(len(yflows)):
            if s < yflows[f][3]:
                rs_step("y", f, s)
        for f in range(len(zflows)):
            if s < zflows[f][3]:
                rs_step("z", f, s)

    long_y, short_y = NY // 2, NY - 1 - NY // 2
    cmine[0] = cpart[y, 0] + cslots[long_y - 1, 0] + cslots[4 + short_y - 1, 0]
    cmine[1] = cpart[y, 1] + cslots[short_y - 1, 1] + cslots[4 + long_y - 1, 1]
    mid = []
    for k, (dx, dz) in enumerate(peers):
        mid.append(
            send(
                cmine.at[lax.rem(x + dx, NX), lax.rem(z + dz, NZ)], cmid.at[k],
                ms_sem.at[k], mr_sem.at[k], at_mid(dx, dz),
            )
        )

    long_z, short_z = NZ // 2, NZ - 1 - NZ // 2
    for half, (right, left_) in enumerate(((long_z, short_z), (short_z, long_z))):
        rows = slice(56 * half, 56 * half + 56)
        total = dpart[z, rows] + dslots[right - 1, rows] + dslots[4 + left_ - 1, rows]
        old = old_x[rows, :]
        new, moved = nesterov(old, mom_x[rows, :], old - total / NZ)
        dfull[z, rows] = new
        dmoved[rows, :] = moved

    ag_copies = {}

    def ag_send(axis, f, s):
        half, q, way, hops = (zflows if axis == "z" else yflows)[f]
        if axis == "z":
            ref = zpiece(dfull, lax.rem(z - way * s + NZ, NZ), half, q)
            ss, rr, target = zas_sem, zar_sem, at_z(way)
        else:
            ref = ypiece(cfull, lax.rem(y - way * s + NY, NY), half, q)
            ss, rr, target = yas_sem, yar_sem, at_y(way)
        ag_copies[axis, f, s] = send(
            ref, ref, ss.at[slot_of(f, s)], rr.at[slot_of(f, s)], target
        )

    def ag_step(axis, f, s):
        hops = (zflows if axis == "z" else yflows)[f][3]
        ag_copies[axis, f, s].wait_recv()
        if s < hops - 1:
            ag_send(axis, f, s + 1)

    for f in range(len(zflows)):
        ag_send("z", f, 0)

    tile = cmine[x, z]
    for k in range(len(peers)):
        mid[k].wait_recv()
        tile = tile + cmid[k]
    ctile[...] = tile
    cfull[y, x, z] = tile
    mid_back = []
    for k, (dx, dz) in enumerate(peers):
        mid_back.append(
            send(ctile, cfull.at[y, x, z], mas_sem.at[k], mar_sem.at[k], at_mid(dx, dz))
        )

    for s in range(NZ // 2):
        for f in range(len(zflows)):
            if s < zflows[f][3]:
                ag_step("z", f, s)

    for copy in mid_back:
        copy.wait_recv()
    for f in range(len(yflows)):
        ag_send("y", f, 0)

    stores = [
        pltpu.make_async_copy(dfull, full_out, store_sem.at[0]),
        pltpu.make_async_copy(dmoved, moved_out, store_sem.at[1]),
    ]
    for copy in stores:
        copy.start()
    for s in range(NY // 2):
        for f in range(len(yflows)):
            if s < yflows[f][3]:
                ag_step("y", f, s)
    for copy in sends:
        copy.wait_send()
    last = pltpu.make_async_copy(cfull, cfull_out, store_sem.at[2])
    last.start()
    for copy in stores:
        copy.wait()
    last.wait()


def finish_kernel(
    full, moved, cfull, eo, ba, cm,
    ai_o, ao_o, fi_o, fo_o, dm_o, sn_o, sm_o, en_o, cm_o,
    ai_x, ao_x, fi_x, fo_x,
):
    b_high, b_low = split_bf16(ba[...])
    left = jnp.concatenate([b_high, b_low, b_high, b_low], axis=1)
    for c in range(NY):
        for j in range(2):
            columns = slice(256 * c + 128 * j, 256 * c + 128 * j + 128)
            coeff = cfull[c, j].reshape(RANK, 128) / NZ
            coeff_moved = momentum_coef * cm[:, columns] + coeff
            cm_o[:, columns] = coeff_moved
            high, low = split_bf16(coeff + momentum_coef * coeff_moved)
            right = jnp.concatenate([high, high, low, low], axis=0)
            product = jnp.dot(left, right, preferred_element_type=F32)
            en_o[:, columns] = eo[:, columns] - outer_rate * product
    unpack(full, (ai_x, ao_x, fi_x, fo_x))
    for which, (src, dst) in enumerate(((ai_x, ai_o), (ao_x, ao_o), (fi_x, fi_o), (fo_x, fo_o))):
        for t in range(TILES[which]):
            size = min(128, WIDTHS[which] - 128 * t)
            dst[:, 128 * t : 128 * t + size] = src[t, :, 0:size]
    for r in range(DENSE_ROWS):
        dm_o[:, 128 * r : 128 * r + 128] = moved[r : r + 1, :]
    sm_o[:, 0:128] = moved[108:109, :]
    sm_o[:, 128:240] = moved[109:110, 0:112]
    for owner in range(NZ):
        sn_o[:, 240 * owner : 240 * owner + 128] = full[owner, 108:109, :]
        sn_o[:, 240 * owner + 128 : 240 * owner + 240] = full[owner, 109:110, 0:112]


def shards(
    attn_in_local,
    attn_out_local,
    ffn_in_local,
    ffn_out_local,
    small_local,
    dense_old,
    dense_momentum,
    small_old,
    small_momentum,
    embed_local,
    embed_old,
    basis,
    coeff_momentum,
):
    any_spec = pl.BlockSpec(memory_space=pl.ANY)
    vmem_spec = pl.BlockSpec(memory_space=pltpu.VMEM)
    dma = pltpu.SemaphoreType.DMA
    tile_scratch = [
        pltpu.VMEM((TILES[i], HEIGHTS[i], 128), F32) for i in range(4)
    ]
    operands = (
        attn_in_local, attn_out_local, ffn_in_local, ffn_out_local, small_local,
        dense_old, dense_momentum, small_old[None, :], small_momentum[None, :],
        embed_local, embed_old, basis,
    )
    nflows = 4 * Q
    full, moved, cfull = pl.pallas_call(
        comm_kernel,
        out_shape=(
            jax.ShapeDtypeStruct((NZ, ROWS, 128), F32),
            jax.ShapeDtypeStruct((ROWS, 128), F32),
            jax.ShapeDtypeStruct((NY, NX, NZ, 8, 128), F32),
        ),
        in_specs=[any_spec] * len(operands),
        out_specs=[any_spec] * 3,
        scratch_shapes=[pltpu.VMEM(a.shape, a.dtype) for a in operands]
        + tile_scratch
        + [
            pltpu.VMEM((ROWS, 128), F32),
            pltpu.VMEM((ROWS, 128), F32),
            pltpu.VMEM((NZ, ROWS, 128), F32),
            pltpu.VMEM((8, ROWS, 128), F32),
            pltpu.VMEM((NZ, ROWS, 128), F32),
            pltpu.VMEM((ROWS, 128), F32),
            pltpu.VMEM((NY, NX, NZ, 8, 128), F32),
            pltpu.VMEM((8, NX, NZ, 8, 128), F32),
            pltpu.VMEM((NX, NZ, 8, 128), F32),
            pltpu.VMEM((NX * NZ - 1, 8, 128), F32),
            pltpu.VMEM((8, 128), F32),
            pltpu.VMEM((NY, NX, NZ, 8, 128), F32),
            dma((len(operands),)),
            dma((3,)),
        ]
        + [dma((nflows * 4,))] * 8
        + [dma((NX * NZ - 1,))] * 4,
        compiler_params=pltpu.CompilerParams(collective_id=0, has_side_effects=True),
        name="exchange",
    )(*operands)

    outs = pl.pallas_call(
        finish_kernel,
        out_shape=(
            jax.ShapeDtypeStruct((48, 576), F32),
            jax.ShapeDtypeStruct((48, 192), F32),
            jax.ShapeDtypeStruct((48, 768), F32),
            jax.ShapeDtypeStruct((192, 192), F32),
            jax.ShapeDtypeStruct((1, 13824), F32),
            jax.ShapeDtypeStruct((1, 1920), F32),
            jax.ShapeDtypeStruct((1, 240), F32),
            jax.ShapeDtypeStruct((48, 2048), F32),
            jax.ShapeDtypeStruct((RANK, 2048), F32),
        ),
        in_specs=[vmem_spec] * 6,
        out_specs=[vmem_spec] * 9,
        scratch_shapes=tile_scratch,
        name="finish",
    )(full, moved, cfull, embed_old, basis, coeff_momentum)
    return (
        outs[0], outs[1], outs[2], outs[3], outs[4],
        outs[5].reshape(-1), outs[6].reshape(-1), outs[7], outs[8],
    )


def solution(mesh):
    placed = (
        P("group", "shard", "tensor"),
        P("group", "shard", "tensor"),
        P("group", "shard", "tensor"),
        P("group", "shard", "tensor"),
        P("group", None),
        P(("shard", "tensor"), "group"),
        P(("shard", "tensor"), "group"),
        P("group"),
        P("group"),
        P("group", "shard", "tensor"),
        P("shard", "tensor"),
        P("shard", None),
        P(None, "tensor"),
    )
    return jax.shard_map(
        shards,
        mesh=mesh,
        in_specs=placed,
        out_specs=(
            P("shard", "tensor"),
            P("shard", "tensor"),
            P("shard", "tensor"),
            P("shard", "tensor"),
            P(("shard", "tensor"), "group"),
            P(),
            P("group"),
            P("shard", "tensor"),
            P(None, "tensor"),
        ),
        check_vma=False,
    )
```

```python
import functools

import jax
import jax.numpy as jnp
from jax import lax
from jax.experimental import pallas as pl
from jax.experimental.pallas import tpu as pltpu
from jax.sharding import PartitionSpec as P

momentum_coef = 0.5
outer_rate = 0.7

MESH = pl.DeviceIdType.MESH
F32 = jnp.float32
BF16 = jnp.bfloat16

NZ = 8
NY = 8
NX = 2
ROWS = 112
DENSE_ROWS = 108
RANK = 64
FAR_FIRST = (4, 3, -3, 2, -2, 1, -1)

PLAN = (
    (0, 0, 0, 24, 0),
    (0, 1, 24, 24, 0),
    (1, 2, 0, 48, 0),
    (2, 2, 0, 6, 72),
    (2, 3, 6, 18, 0),
    (2, 4, 24, 18, 0),
    (2, 5, 42, 6, 0),
    (3, 5, 0, 48, 36),
    (3, 6, 48, 72, 0),
    (3, 7, 120, 72, 0),
)
WIDTHS = (576, 192, 768, 192)
HEIGHTS = (48, 48, 48, 192)
TILES = tuple(-(-width // 128) for width in WIDTHS)


def nesterov(old_value, momentum, delta):
    moved = momentum_coef * momentum + delta
    return (old_value - outer_rate * (delta + momentum_coef * moved), moved)


def lower_lanes(shape):
    return lax.broadcasted_iota(jnp.int32, shape, 1) < 64


def pack(tiles, flat):
    for which, owner, row, count, base in PLAN:
        xs = tiles[which]
        full = WIDTHS[which] // 128
        if WIDTHS[which] % 128 == 0:
            for t in range(full):
                flat[owner, pl.ds(base + t, count, stride=full), :] = xs[t, pl.ds(row, count), :]
            continue
        n, step = count // 2, 2 * full + 1
        low = lower_lanes((n, 128))
        even = [xs[t, pl.ds(row, n, stride=2), :] for t in range(full + 1)]
        turned = [
            pltpu.roll(xs[t, pl.ds(row + 1, n, stride=2), :], 64, 1) for t in range(full + 1)
        ]
        for t in range(full):
            flat[owner, pl.ds(base + t, n, stride=step), :] = even[t]
        flat[owner, pl.ds(base + full, n, stride=step), :] = jnp.where(low, even[full], turned[0])
        for t in range(full):
            flat[owner, pl.ds(base + full + 1 + t, n, stride=step), :] = jnp.where(
                low, turned[t], turned[t + 1]
            )


def unpack(flat, tiles):
    for which, owner, row, count, base in PLAN:
        xs = tiles[which]
        full = WIDTHS[which] // 128
        if WIDTHS[which] % 128 == 0:
            for t in range(full):
                xs[t, pl.ds(row, count), :] = flat[owner, pl.ds(base + t, count, stride=full), :]
            continue
        n, step = count // 2, 2 * full + 1
        low = lower_lanes((n, 128))
        rows = [flat[owner, pl.ds(base + t, n, stride=step), :] for t in range(step)]
        for t in range(full + 1):
            xs[t, pl.ds(row, n, stride=2), :] = rows[t]
        for t in range(full):
            xs[t, pl.ds(row + 1, n, stride=2), :] = pltpu.roll(
                jnp.where(low, rows[full + 1 + t], rows[full + t]), 64, 1
            )
        xs[full, pl.ds(row + 1, n, stride=2), :] = pltpu.roll(rows[2 * full], 64, 1)


def split_bf16(value):
    high = value.astype(BF16)
    return high, (value - high.astype(F32)).astype(BF16)


def comm_kernel(*refs):
    (ai, ao, fi, fo, sl, dold, dmom, sold, smom, el, eo, ba) = refs[:12]
    full_out, moved_out, cfull_out = refs[12:15]
    (
        ai_v, ao_v, fi_v, fo_v, sl_v, dold_v, dmom_v, sold_v, smom_v, el_v, eo_v, ba_v,
        ai_x, ao_x, fi_x, fo_x, old_x, mom_x,
        dpart, dslots, dfull, dmoved,
        cpart, cslots, cmine, cmid, ctile, cfull,
        load_sem, store_sem,
        zs_sem, zr_sem, zas_sem, zar_sem,
        ys_sem, yr_sem, yas_sem, yar_sem,
        ms_sem, mr_sem, mas_sem, mar_sem,
    ) = refs[15:]

    z = lax.axis_index("group")
    shard = lax.axis_index("shard")
    y = shard // NX
    x = lax.rem(shard, NX)

    def at_z(offset):
        return {"group": lax.rem(z + offset + NZ, NZ)}

    def at_y(offset):
        return {"shard": lax.rem(y + offset + NY, NY) * NX + x}

    def at_mid(dx, dz):
        return {"group": lax.rem(z + dz + NZ, NZ), "shard": y * NX + lax.rem(x + dx, NX)}

    peers = [(dx, dz) for dz in FAR_FIRST for dx in (1, 0)] + [(1, 0)]

    loads = []
    for i, (src, dst) in enumerate(
        (
            (el, el_v), (eo, eo_v), (ba, ba_v), (ai, ai_v), (ao, ao_v), (fi, fi_v), (fo, fo_v),
            (sl, sl_v), (dold, dold_v), (dmom, dmom_v), (sold, sold_v), (smom, smom_v),
        )
    ):
        copy = pltpu.make_async_copy(src, dst, load_sem.at[i])
        copy.start()
        loads.append(copy)

    barrier = pltpu.get_barrier_semaphore()
    greeted = [at_y(offset) for offset in FAR_FIRST] + [at_mid(dx, dz) for dx, dz in peers]
    for peer in greeted:
        pl.semaphore_signal(barrier, inc=1, device_id=peer, device_id_type=MESH)

    sends = []

    def send(src, dst, send_sem, recv_sem, device):
        copy = pltpu.make_async_remote_copy(
            src_ref=src, dst_ref=dst, send_sem=send_sem, recv_sem=recv_sem,
            device_id=device, device_id_type=MESH,
        )
        copy.start()
        sends.append(copy)
        return copy

    for copy in loads[:3]:
        copy.wait()
    b_high, b_low = split_bf16(ba_v[...])
    left = jnp.concatenate([b_high, b_low, b_high, b_low], axis=0)

    y_rs = []
    for k, offset in enumerate(FAR_FIRST + (0,)):
        c = lax.rem(y + offset + NY, NY)
        columns = pl.ds(pl.multiple_of(c * 256, 256), 256)
        high, low = split_bf16(eo_v[:, columns] - el_v[0, :, columns].astype(F32))
        right = jnp.concatenate([high, high, low, low], axis=0)
        product = lax.dot_general(
            left, right, (((0,), (0,)), ((), ())), preferred_element_type=F32
        )
        cpart[c, 0] = product[:, :128].reshape(NZ, 8, 128)
        cpart[c, 1] = product[:, 128:].reshape(NZ, 8, 128)
        if k == 0:
            pl.semaphore_wait(barrier, len(greeted))
        if offset:
            y_rs.append(
                send(cpart.at[c], cslots.at[k], ys_sem.at[k], yr_sem.at[k], at_y(offset))
            )

    for copy in loads[3:]:
        copy.wait()
    for which, (src, dst) in enumerate(
        ((ai_v, ai_x), (ao_v, ao_x), (fi_v, fi_x), (fo_v, fo_x))
    ):
        for t in range(TILES[which]):
            size = min(128, WIDTHS[which] - 128 * t)
            dst[t, :, 0:size] = src[0, :, 128 * t : 128 * t + size].astype(F32)
    pack((ai_x, ao_x, fi_x, fo_x), dpart)
    small = sl_v[...].astype(F32)
    for owner in range(NZ):
        dpart[owner, 104:112, :] = jnp.where(
            lax.broadcasted_iota(jnp.int32, (8, 128), 0) < 4, dpart[owner, 104:112, :], 0.0
        )
        dpart[owner, 108:109, :] = small[:, 240 * owner : 240 * owner + 128]
        dpart[owner, 109:110, 0:112] = small[:, 240 * owner + 128 : 240 * owner + 240]

    z_rs = []
    for k, offset in enumerate(FAR_FIRST):
        src = dpart.at[lax.rem(z + offset + NZ, NZ)]
        z_rs.append(send(src, dslots.at[k], zs_sem.at[k], zr_sem.at[k], at_z(offset)))

    for src, dst, small_src in ((dold_v, old_x, sold_v), (dmom_v, mom_x, smom_v)):
        dst[104:112, :] = jnp.zeros((8, 128), F32)
        for r in range(DENSE_ROWS):
            dst[r : r + 1, :] = src[:, 128 * r : 128 * r + 128]
        dst[108:109, :] = small_src[:, 0:128]
        dst[109:110, 0:112] = small_src[:, 128:240]

    for copy in y_rs:
        copy.wait_recv()
    for j in range(NX):
        total = cpart[y, j]
        for k in range(len(y_rs)):
            total = total + cslots[k, j]
        cmine[j] = total
    mid = []
    for k, (dx, dz) in enumerate(peers):
        mid.append(
            send(
                cmine.at[lax.rem(x + dx, NX), lax.rem(z + dz + NZ, NZ)], cmid.at[k],
                ms_sem.at[k], mr_sem.at[k], at_mid(dx, dz),
            )
        )

    for copy in z_rs:
        copy.wait_recv()
    total = dpart[z]
    for k in range(len(z_rs)):
        total = total + dslots[k]
    old = old_x[...]
    new, moved = nesterov(old, mom_x[...], old - total / NZ)
    dfull[z] = new
    dmoved[...] = moved

    z_ag = {}

    def dense_send(k, offset):
        z_ag[k] = send(dfull.at[z], dfull.at[z], zas_sem.at[k], zar_sem.at[k], at_z(offset))

    for k, offset in enumerate(FAR_FIRST):
        if abs(offset) < 3:
            dense_send(k, offset)

    for copy in mid:
        copy.wait_recv()
    tile = cmine[x, z]
    for k in range(len(peers)):
        tile = tile + cmid[k]
    ctile[...] = tile
    cfull[y, x, z] = tile
    mid_back = []
    for k, (dx, dz) in enumerate(peers):
        mid_back.append(
            send(ctile, cfull.at[y, x, z], mas_sem.at[k], mar_sem.at[k], at_mid(dx, dz))
        )
    for k, offset in enumerate(FAR_FIRST):
        if abs(offset) >= 3:
            dense_send(k, offset)

    for copy in mid_back:
        copy.wait_recv()
    y_ag = []
    for k, offset in enumerate(FAR_FIRST):
        y_ag.append(send(cfull.at[y], cfull.at[y], yas_sem.at[k], yar_sem.at[k], at_y(offset)))

    stores = [pltpu.make_async_copy(dmoved, moved_out, store_sem.at[0])]
    stores[0].start()
    copy = pltpu.make_async_copy(cfull.at[y], cfull_out.at[y], store_sem.at[2])
    copy.start()
    stores.append(copy)
    for k in range(len(FAR_FIRST)):
        z_ag[k].wait_recv()
    copy = pltpu.make_async_copy(dfull, full_out, store_sem.at[1])
    copy.start()
    stores.append(copy)
    for k in (5, 6, 3, 4, 1, 2, 0):
        y_ag[k].wait_recv()
        c = lax.rem(y - FAR_FIRST[k] + NY, NY)
        copy = pltpu.make_async_copy(cfull.at[c], cfull_out.at[c], store_sem.at[3 + k])
        copy.start()
        stores.append(copy)
    for copy in sends:
        copy.wait_send()
    for copy in stores:
        copy.wait()


def finish_kernel(
    full, moved, cfull, eo, ba, cm,
    ai_o, ao_o, fi_o, fo_o, dm_o, sn_o, sm_o, en_o, cm_o,
    ai_x, ao_x, fi_x, fo_x, sn_x,
):
    b_high, b_low = split_bf16(ba[...])
    left = jnp.concatenate([b_high, b_low, b_high, b_low], axis=1)
    for c in range(NY):
        for j in range(2):
            columns = slice(256 * c + 128 * j, 256 * c + 128 * j + 128)
            coeff = cfull[c, j].reshape(RANK, 128) / NZ
            coeff_moved = momentum_coef * cm[:, columns] + coeff
            cm_o[:, columns] = coeff_moved
            high, low = split_bf16(coeff + momentum_coef * coeff_moved)
            right = jnp.concatenate([high, high, low, low], axis=0)
            product = jnp.dot(left, right, preferred_element_type=F32)
            en_o[:, columns] = eo[:, columns] - outer_rate * product
    unpack(full, (ai_x, ao_x, fi_x, fo_x))
    for which, (src, dst) in enumerate(((ai_x, ai_o), (ao_x, ao_o), (fi_x, fi_o), (fo_x, fo_o))):
        for t in range(TILES[which]):
            size = min(128, WIDTHS[which] - 128 * t)
            dst[:, 128 * t : 128 * t + size] = src[t, :, 0:size]
    for r in range(DENSE_ROWS):
        dm_o[:, 128 * r : 128 * r + 128] = moved[r : r + 1, :]
    sm_o[:, 0:128] = moved[108:109, :]
    sm_o[:, 128:240] = moved[109:110, 0:112]
    for owner in range(NZ):
        sn_x[:, 240 * owner : 240 * owner + 128] = full[owner, 108:109, :]
        sn_x[:, 240 * owner + 128 : 240 * owner + 240] = full[owner, 109:110, 0:112]
    for r in range(15):
        sn_o[r : r + 1, :] = sn_x[:, 128 * r : 128 * r + 128]


def shards(
    attn_in_local,
    attn_out_local,
    ffn_in_local,
    ffn_out_local,
    small_local,
    dense_old,
    dense_momentum,
    small_old,
    small_momentum,
    embed_local,
    embed_old,
    basis,
    coeff_momentum,
):
    any_spec = pl.BlockSpec(memory_space=pl.ANY)
    vmem_spec = pl.BlockSpec(memory_space=pltpu.VMEM)
    dma = pltpu.SemaphoreType.DMA
    tile_scratch = [
        pltpu.VMEM((TILES[i], HEIGHTS[i], 128), F32) for i in range(4)
    ]
    operands = (
        attn_in_local, attn_out_local, ffn_in_local, ffn_out_local, small_local,
        dense_old, dense_momentum, small_old[None, :], small_momentum[None, :],
        embed_local, embed_old, basis,
    )
    full, moved, cfull = pl.pallas_call(
        comm_kernel,
        out_shape=(
            jax.ShapeDtypeStruct((NZ, ROWS, 128), F32),
            jax.ShapeDtypeStruct((ROWS, 128), F32),
            jax.ShapeDtypeStruct((NY, NX, NZ, 8, 128), F32),
        ),
        in_specs=[any_spec] * len(operands),
        out_specs=[any_spec] * 3,
        scratch_shapes=[pltpu.VMEM(a.shape, a.dtype) for a in operands]
        + tile_scratch
        + [
            pltpu.VMEM((ROWS, 128), F32),
            pltpu.VMEM((ROWS, 128), F32),
            pltpu.VMEM((NZ, ROWS, 128), F32),
            pltpu.VMEM((NZ - 1, ROWS, 128), F32),
            pltpu.VMEM((NZ, ROWS, 128), F32),
            pltpu.VMEM((ROWS, 128), F32),
            pltpu.VMEM((NY, NX, NZ, 8, 128), F32),
            pltpu.VMEM((NY - 1, NX, NZ, 8, 128), F32),
            pltpu.VMEM((NX, NZ, 8, 128), F32),
            pltpu.VMEM((NX * NZ - 1, 8, 128), F32),
            pltpu.VMEM((8, 128), F32),
            pltpu.VMEM((NY, NX, NZ, 8, 128), F32),
            dma((len(operands),)),
            dma((10,)),
        ]
        + [dma((7,))] * 8
        + [dma((NX * NZ - 1,))] * 4,
        compiler_params=pltpu.CompilerParams(collective_id=0, has_side_effects=True),
        name="exchange",
    )(*operands)

    outs = pl.pallas_call(
        finish_kernel,
        out_shape=(
            jax.ShapeDtypeStruct((48, 576), F32),
            jax.ShapeDtypeStruct((48, 192), F32),
            jax.ShapeDtypeStruct((48, 768), F32),
            jax.ShapeDtypeStruct((192, 192), F32),
            jax.ShapeDtypeStruct((1, 13824), F32),
            jax.ShapeDtypeStruct((15, 128), F32),
            jax.ShapeDtypeStruct((1, 240), F32),
            jax.ShapeDtypeStruct((48, 2048), F32),
            jax.ShapeDtypeStruct((RANK, 2048), F32),
        ),
        in_specs=[vmem_spec] * 6,
        out_specs=[vmem_spec] * 9,
        scratch_shapes=tile_scratch + [pltpu.VMEM((1, 1920), F32)],
        name="finish",
    )(full, moved, cfull, embed_old, basis, coeff_momentum)
    return (
        outs[0], outs[1], outs[2], outs[3], outs[4],
        outs[5].reshape(-1), outs[6].reshape(-1), outs[7], outs[8],
    )


def solution(mesh):
    placed = (
        P("group", "shard", "tensor"),
        P("group", "shard", "tensor"),
        P("group", "shard", "tensor"),
        P("group", "shard", "tensor"),
        P("group", None),
        P(("shard", "tensor"), "group"),
        P(("shard", "tensor"), "group"),
        P("group"),
        P("group"),
        P("group", "shard", "tensor"),
        P("shard", "tensor"),
        P("shard", None),
        P(None, "tensor"),
    )
    return jax.shard_map(
        shards,
        mesh=mesh,
        in_specs=placed,
        out_specs=(
            P("shard", "tensor"),
            P("shard", "tensor"),
            P("shard", "tensor"),
            P("shard", "tensor"),
            P(("shard", "tensor"), "group"),
            P(),
            P("group"),
            P("shard", "tensor"),
            P(None, "tensor"),
        ),
        check_vma=False,
    )
```

```python
import functools

import jax
import jax.numpy as jnp
from jax import lax
from jax.experimental import pallas as pl
from jax.experimental.pallas import tpu as pltpu
from jax.sharding import PartitionSpec as P

momentum_coef = 0.5
outer_rate = 0.7

MESH = pl.DeviceIdType.MESH
F32 = jnp.float32
BF16 = jnp.bfloat16

NZ = 8
NY = 8
NX = 2
ROWS = 112
DENSE_ROWS = 108
RANK = 64
FAR_FIRST = (4, 3, -3, 2, -2, 1, -1)
NEAR = (3, 4, 5, 6)
VIA_IN = ()
VIA_OUT = (4, 3, -3, 2, -2)

PLAN = (
    (0, 0, 0, 24, 0),
    (0, 1, 24, 24, 0),
    (1, 2, 0, 48, 0),
    (2, 2, 0, 6, 72),
    (2, 3, 6, 18, 0),
    (2, 4, 24, 18, 0),
    (2, 5, 42, 6, 0),
    (3, 5, 0, 48, 36),
    (3, 6, 48, 72, 0),
    (3, 7, 120, 72, 0),
)
WIDTHS = (576, 192, 768, 192)
HEIGHTS = (48, 48, 48, 192)
TILES = tuple(-(-width // 128) for width in WIDTHS)


def nesterov(old_value, momentum, delta):
    moved = momentum_coef * momentum + delta
    return (old_value - outer_rate * (delta + momentum_coef * moved), moved)


def lower_lanes(shape):
    return lax.broadcasted_iota(jnp.int32, shape, 1) < 64


def pack(tiles, flat):
    for which, owner, row, count, base in PLAN:
        xs = tiles[which]
        full = WIDTHS[which] // 128
        if WIDTHS[which] % 128 == 0:
            for t in range(full):
                flat[owner, pl.ds(base + t, count, stride=full), :] = xs[t, pl.ds(row, count), :]
            continue
        n, step = count // 2, 2 * full + 1
        low = lower_lanes((n, 128))
        even = [xs[t, pl.ds(row, n, stride=2), :] for t in range(full + 1)]
        turned = [
            pltpu.roll(xs[t, pl.ds(row + 1, n, stride=2), :], 64, 1) for t in range(full + 1)
        ]
        for t in range(full):
            flat[owner, pl.ds(base + t, n, stride=step), :] = even[t]
        flat[owner, pl.ds(base + full, n, stride=step), :] = jnp.where(low, even[full], turned[0])
        for t in range(full):
            flat[owner, pl.ds(base + full + 1 + t, n, stride=step), :] = jnp.where(
                low, turned[t], turned[t + 1]
            )


def unpack(flat, tiles):
    for which, owner, row, count, base in PLAN:
        xs = tiles[which]
        full = WIDTHS[which] // 128
        if WIDTHS[which] % 128 == 0:
            for t in range(full):
                xs[t, pl.ds(row, count), :] = flat[owner, pl.ds(base + t, count, stride=full), :]
            continue
        n, step = count // 2, 2 * full + 1
        low = lower_lanes((n, 128))
        rows = [flat[owner, pl.ds(base + t, n, stride=step), :] for t in range(step)]
        for t in range(full + 1):
            xs[t, pl.ds(row, n, stride=2), :] = rows[t]
        for t in range(full):
            xs[t, pl.ds(row + 1, n, stride=2), :] = pltpu.roll(
                jnp.where(low, rows[full + 1 + t], rows[full + t]), 64, 1
            )
        xs[full, pl.ds(row + 1, n, stride=2), :] = pltpu.roll(rows[2 * full], 64, 1)


def split_bf16(value):
    high = value.astype(BF16)
    return high, (value - high.astype(F32)).astype(BF16)


def comm_kernel(*refs):
    (ai, ao, fi, fo, sl, dold, dmom, sold, smom, el, eo, ba) = refs[:12]
    full_out, moved_out, cfull_out = refs[12:15]
    (
        ai_v, ao_v, fi_v, fo_v, sl_v, dold_v, dmom_v, sold_v, smom_v, el_v, eo_v, ba_v,
        ai_x, ao_x, fi_x, fo_x, old_x, mom_x,
        dpart, dslots, dfull, dmoved,
        cpart, cslots, xslots, cmine, ctiles, cfull,
        load_sem, store_sem,
        zs_sem, zr_sem, zas_sem, zar_sem,
        ys_sem, yr_sem, yas_sem, yar_sem,
        ms_sem, mr_sem, mas_sem, mar_sem,
    ) = refs[15:]

    z = lax.axis_index("group")
    shard = lax.axis_index("shard")
    y = shard // NX
    x = lax.rem(shard, NX)

    def at_z(offset):
        return {"group": lax.rem(z + offset + NZ, NZ)}

    def at_yx(dy, dx):
        return {"shard": lax.rem(y + dy + NY, NY) * NX + lax.rem(x + dx, NX)}

    peers = [(dy, dx) for dy in FAR_FIRST for dx in (1, 0)] + [(0, 1)]

    loads = []
    for i, (src, dst) in enumerate(
        (
            (el, el_v), (eo, eo_v), (ba, ba_v), (ai, ai_v), (ao, ao_v), (fi, fi_v), (fo, fo_v),
            (sl, sl_v), (dold, dold_v), (dmom, dmom_v), (sold, sold_v), (smom, smom_v),
        )
    ):
        copy = pltpu.make_async_copy(src, dst, load_sem.at[i])
        copy.start()
        loads.append(copy)

    barrier = pltpu.get_barrier_semaphore()
    greeted = [at_yx(dy, dx) for dy, dx in peers] + [at_z(offset) for offset in FAR_FIRST]
    for peer in greeted:
        pl.semaphore_signal(barrier, inc=1, device_id=peer, device_id_type=MESH)

    sends = []

    def send(src, dst, send_sem, recv_sem, device):
        copy = pltpu.make_async_remote_copy(
            src_ref=src, dst_ref=dst, send_sem=send_sem, recv_sem=recv_sem,
            device_id=device, device_id_type=MESH,
        )
        copy.start()
        sends.append(copy)
        return copy

    for copy in loads[:3]:
        copy.wait()
    b_high, b_low = split_bf16(ba_v[...])
    left = jnp.concatenate([b_high, b_low, b_high, b_low], axis=0)

    rs, halves = [], {}
    for offset in FAR_FIRST + (0,):
        c = lax.rem(y + offset + NY, NY)
        columns = pl.ds(pl.multiple_of(c * 256, 256), 256)
        high, low = split_bf16(eo_v[:, columns] - el_v[0, :, columns].astype(F32))
        right = jnp.concatenate([high, high, low, low], axis=0)
        product = lax.dot_general(
            left, right, (((0,), (0,)), ((), ())), preferred_element_type=F32
        )
        cpart[c, 0] = product[:, :128].reshape(NZ, 8, 128)
        cpart[c, 1] = product[:, 128:].reshape(NZ, 8, 128)
        if offset == FAR_FIRST[0]:
            pl.semaphore_wait(barrier, len(greeted))
        for k, (dy, dx) in enumerate(peers):
            if dy == offset and dy in VIA_IN:
                if dx:
                    halves[dy] = send(
                        cpart.at[c, 1 - x], xslots.at[VIA_IN.index(dy)],
                        ys_sem.at[k], yr_sem.at[k], at_yx(0, 1),
                    )
            elif dy == offset:
                src = cpart.at[c, lax.rem(x + dx, NX)]
                rs.append(send(src, cslots.at[k], ys_sem.at[k], yr_sem.at[k], at_yx(dy, dx)))

    for copy in loads[3:]:
        copy.wait()
    for which, (src, dst) in enumerate(
        ((ai_v, ai_x), (ao_v, ao_x), (fi_v, fi_x), (fo_v, fo_x))
    ):
        for t in range(TILES[which]):
            size = min(128, WIDTHS[which] - 128 * t)
            dst[t, :, 0:size] = src[0, :, 128 * t : 128 * t + size].astype(F32)
    pack((ai_x, ao_x, fi_x, fo_x), dpart)
    small = sl_v[...].astype(F32)
    for owner in range(NZ):
        dpart[owner, 104:112, :] = jnp.where(
            lax.broadcasted_iota(jnp.int32, (8, 128), 0) < 4, dpart[owner, 104:112, :], 0.0
        )
        dpart[owner, 108:109, :] = small[:, 240 * owner : 240 * owner + 128]
        dpart[owner, 109:110, 0:112] = small[:, 240 * owner + 128 : 240 * owner + 240]

    z_rs = []
    for k, offset in enumerate(FAR_FIRST):
        src = dpart.at[lax.rem(z + offset + NZ, NZ)]
        z_rs.append(send(src, dslots.at[k], zs_sem.at[k], zr_sem.at[k], at_z(offset)))

    for k, (dy, dx) in enumerate(peers):
        if dy in VIA_IN and not dx:
            halves[dy].wait_recv()
            c = lax.rem(y + dy + NY, NY)
            cpart[c, x] = cpart[c, x] + xslots[VIA_IN.index(dy)]
            rs.append(
                send(cpart.at[c, x], cslots.at[k], ys_sem.at[k], yr_sem.at[k], at_yx(dy, 0))
            )

    for src, dst, small_src in ((dold_v, old_x, sold_v), (dmom_v, mom_x, smom_v)):
        dst[104:112, :] = jnp.zeros((8, 128), F32)
        for r in range(DENSE_ROWS):
            dst[r : r + 1, :] = src[:, 128 * r : 128 * r + 128]
        dst[108:109, :] = small_src[:, 0:128]
        dst[109:110, 0:112] = small_src[:, 128:240]

    for copy in rs:
        copy.wait_recv()
    total = cpart[y, x]
    for k, (dy, dx) in enumerate(peers):
        if not (dx and dy in VIA_IN):
            total = total + cslots[k]
    cmine[...] = total
    tiles = []
    for k, offset in enumerate(FAR_FIRST):
        src = cmine.at[lax.rem(z + offset + NZ, NZ)]
        tiles.append(send(src, ctiles.at[k], ms_sem.at[k], mr_sem.at[k], at_z(offset)))

    for copy in z_rs:
        copy.wait_recv()
    total = dpart[z]
    for k in range(len(z_rs)):
        total = total + dslots[k]
    old = old_x[...]
    new, moved = nesterov(old, mom_x[...], old - total / NZ)
    dfull[z] = new
    dmoved[...] = moved
    z_ag = []

    def dense_send(k):
        z_ag.append(
            send(dfull.at[z], dfull.at[z], zas_sem.at[k], zar_sem.at[k], at_z(FAR_FIRST[k]))
        )

    for k in NEAR:
        dense_send(k)

    for copy in tiles:
        copy.wait_recv()
    total = cmine[z]
    for k in range(len(tiles)):
        total = total + ctiles[k]
    cfull[y, x, z] = total
    tile = cfull.at[y, x, z]
    tiles_back = []
    for k, offset in enumerate(FAR_FIRST):
        tiles_back.append(send(tile, tile, mas_sem.at[k], mar_sem.at[k], at_z(offset)))
    for k in range(NZ - 1):
        if k not in NEAR:
            dense_send(k)
    for copy in tiles_back:
        copy.wait_recv()
    ag = {}

    def pass_on(k, c, j, device):
        block = cfull.at[c, j]
        ag[peers[k]] = send(block, block, yas_sem.at[k], yar_sem.at[k], device)

    for straight in (0, 1):
        for k, (dy, dx) in enumerate(peers):
            if dx == straight and not (dx and dy in VIA_OUT):
                pass_on(k, y, x, at_yx(dy, dx))

    stores = []

    def store(src, dst):
        copy = pltpu.make_async_copy(src, dst, store_sem.at[len(stores)])
        copy.start()
        stores.append(copy)

    store(dmoved, moved_out)
    store(cfull.at[y, x], cfull_out.at[y, x])
    def arrive(dy, dx):
        ag[dy, dx].wait_recv()
        c, j = lax.rem(y - dy + NY, NY), lax.rem(x + dx, NX)
        store(cfull.at[c, j], cfull_out.at[c, j])
        return c

    for dy in reversed(VIA_OUT):
        c = arrive(dy, 0)
        pass_on(peers.index((dy, 1)), c, x, at_yx(0, 1))
    for dy, dx in reversed(peers):
        if dy not in VIA_OUT:
            arrive(dy, dx)
    for copy in z_ag:
        copy.wait_recv()
    store(dfull, full_out)
    for dy in reversed(VIA_OUT):
        arrive(dy, 1)
    for copy in sends:
        copy.wait_send()
    for copy in stores:
        copy.wait()


def finish_kernel(*refs):
    sources, targets = refs[:6], refs[6:15]
    full, moved, cfull, eo, ba, cm = refs[15:21]
    ai_o, ao_o, fi_o, fo_o, dm_o, sn_o, sm_o, en_o, cm_o = refs[21:30]
    ai_x, ao_x, fi_x, fo_x, sn_x, load_sem, store_sem = refs[30:]

    loads = []
    for i, ref in enumerate((full, moved, cfull, eo, ba, cm)):
        copy = pltpu.make_async_copy(sources[i], ref, load_sem.at[i])
        copy.start()
        loads.append(copy)
    stores = []

    def store(src, dst):
        copy = pltpu.make_async_copy(src, dst, store_sem.at[len(stores)])
        copy.start()
        stores.append(copy)

    loads[0].wait()
    unpack(full, (ai_x, ao_x, fi_x, fo_x))
    for which, (src, dst) in enumerate(((ai_x, ai_o), (ao_x, ao_o), (fi_x, fi_o), (fo_x, fo_o))):
        for t in range(TILES[which]):
            size = min(128, WIDTHS[which] - 128 * t)
            dst[:, 128 * t : 128 * t + size] = src[t, :, 0:size]
        store(dst, targets[which])
    loads[1].wait()
    for r in range(DENSE_ROWS):
        dm_o[:, 128 * r : 128 * r + 128] = moved[r : r + 1, :]
    store(dm_o, targets[4])
    sm_o[:, 0:128] = moved[108:109, :]
    sm_o[:, 128:240] = moved[109:110, 0:112]
    store(sm_o, targets[6])
    for owner in range(NZ):
        sn_x[:, 240 * owner : 240 * owner + 128] = full[owner, 108:109, :]
        sn_x[:, 240 * owner + 128 : 240 * owner + 240] = full[owner, 109:110, 0:112]
    for r in range(15):
        sn_o[r : r + 1, :] = sn_x[:, 128 * r : 128 * r + 128]
    store(sn_o, targets[5])
    for copy in loads[2:]:
        copy.wait()
    b_high, b_low = split_bf16(ba[...])
    left = jnp.concatenate([b_high, b_low, b_high, b_low], axis=1)
    for c in range(NY):
        columns = slice(256 * c, 256 * c + 256)
        coeff = jnp.concatenate([cfull[c, j].reshape(RANK, 128) for j in range(2)], axis=1) / NZ
        coeff_moved = momentum_coef * cm[:, columns] + coeff
        cm_o[:, columns] = coeff_moved
        high, low = split_bf16(coeff + momentum_coef * coeff_moved)
        right = jnp.concatenate([high, high, low, low], axis=0)
        product = jnp.dot(left, right, preferred_element_type=F32)
        en_o[:, columns] = eo[:, columns] - outer_rate * product
        if c % 2:
            columns = slice(256 * c - 256, 256 * c + 256)
            store(cm_o.at[:, columns], targets[8].at[:, columns])
            store(en_o.at[:, columns], targets[7].at[:, columns])
    for copy in stores:
        copy.wait()


def shards(
    attn_in_local,
    attn_out_local,
    ffn_in_local,
    ffn_out_local,
    small_local,
    dense_old,
    dense_momentum,
    small_old,
    small_momentum,
    embed_local,
    embed_old,
    basis,
    coeff_momentum,
):
    any_spec = pl.BlockSpec(memory_space=pl.ANY)
    dma = pltpu.SemaphoreType.DMA
    tile_scratch = [
        pltpu.VMEM((TILES[i], HEIGHTS[i], 128), F32) for i in range(4)
    ]
    operands = (
        attn_in_local, attn_out_local, ffn_in_local, ffn_out_local, small_local,
        dense_old, dense_momentum, small_old[None, :], small_momentum[None, :],
        embed_local, embed_old, basis,
    )
    full, moved, cfull = pl.pallas_call(
        comm_kernel,
        out_shape=(
            jax.ShapeDtypeStruct((NZ, ROWS, 128), F32),
            jax.ShapeDtypeStruct((ROWS, 128), F32),
            jax.ShapeDtypeStruct((NY, NX, NZ, 8, 128), F32),
        ),
        in_specs=[any_spec] * len(operands),
        out_specs=[any_spec] * 3,
        scratch_shapes=[pltpu.VMEM(a.shape, a.dtype) for a in operands]
        + tile_scratch
        + [
            pltpu.VMEM((ROWS, 128), F32),
            pltpu.VMEM((ROWS, 128), F32),
            pltpu.VMEM((NZ, ROWS, 128), F32),
            pltpu.VMEM((NZ - 1, ROWS, 128), F32),
            pltpu.VMEM((NZ, ROWS, 128), F32),
            pltpu.VMEM((ROWS, 128), F32),
            pltpu.VMEM((NY, NX, NZ, 8, 128), F32),
            pltpu.VMEM((NY * NX - 1, NZ, 8, 128), F32),
            pltpu.VMEM((max(1, len(VIA_IN)), NZ, 8, 128), F32),
            pltpu.VMEM((NZ, 8, 128), F32),
            pltpu.VMEM((NZ - 1, 8, 128), F32),
            pltpu.VMEM((NY, NX, NZ, 8, 128), F32),
            dma((len(operands),)),
            dma((NY * NX + 2,)),
        ]
        + [dma((NZ - 1,))] * 4
        + [dma((NY * NX - 1,))] * 4
        + [dma((NZ - 1,))] * 4,
        compiler_params=pltpu.CompilerParams(collective_id=0, has_side_effects=True),
        name="exchange",
    )(*operands)

    finish_args = (full, moved, cfull, embed_old, basis, coeff_momentum)
    results = (
        (48, 576), (48, 192), (48, 768), (192, 192), (1, 13824), (15, 128), (1, 240),
        (48, 2048), (RANK, 2048),
    )
    outs = pl.pallas_call(
        finish_kernel,
        out_shape=[jax.ShapeDtypeStruct(shape, F32) for shape in results],
        in_specs=[any_spec] * len(finish_args),
        out_specs=[any_spec] * len(results),
        scratch_shapes=[pltpu.VMEM(a.shape, F32) for a in finish_args]
        + [pltpu.VMEM(shape, F32) for shape in results]
        + tile_scratch
        + [pltpu.VMEM((1, 1920), F32), dma((len(finish_args),)), dma((15,))],
        name="finish",
    )(*finish_args)
    return (
        outs[0], outs[1], outs[2], outs[3], outs[4],
        outs[5].reshape(-1), outs[6].reshape(-1), outs[7], outs[8],
    )


def solution(mesh):
    placed = (
        P("group", "shard", "tensor"),
        P("group", "shard", "tensor"),
        P("group", "shard", "tensor"),
        P("group", "shard", "tensor"),
        P("group", None),
        P(("shard", "tensor"), "group"),
        P(("shard", "tensor"), "group"),
        P("group"),
        P("group"),
        P("group", "shard", "tensor"),
        P("shard", "tensor"),
        P("shard", None),
        P(None, "tensor"),
    )
    return jax.shard_map(
        shards,
        mesh=mesh,
        in_specs=placed,
        out_specs=(
            P("shard", "tensor"),
            P("shard", "tensor"),
            P("shard", "tensor"),
            P("shard", "tensor"),
            P(("shard", "tensor"), "group"),
            P(),
            P("group"),
            P("shard", "tensor"),
            P(None, "tensor"),
        ),
        check_vma=False,
    )
```
